32 devices in a mesh: groups: 2 (over x), tm: 16 (over z, y, core).
Axes of the slice: x: 2, y: 2, z: 4, core: 2. Of those that a mesh axis runs over, the one named last changes fastest.
Arguments:
- receptance: bfloat16 [4096, 1024], P(('groups', 'tm')), parts along dimension 0, may hold values from -0.75 to 0.75
- key_input: bfloat16 [4096, 1024], P(('groups', 'tm')), parts along dimension 0, may hold values from -6 to 6
- values: bfloat16 [4096, 1024], P(('groups', 'tm')), parts along dimension 0, may hold values from -6 to 6
- log_decay: bfloat16 [4096, 1024], P(('groups', 'tm')), parts along dimension 0, may hold values from -1 to 0
- kappa_raw: bfloat16 [4096, 1024], P(('groups', 'tm')), parts along dimension 0, may hold values from -6 to 6
- removal: bfloat16 [4096, 1024], P(('groups', 'tm')), parts along dimension 0, may hold values from 0 to 1
- initial_state: float32 [32, 64, 64], P('groups'), parts along dimension 0, may hold values from -3 to 3
- out_weight: bfloat16 [1024, 1024], replicated, may hold values from -0.1875 to 0.1875
- grad_output: bfloat16 [1024, 4096], P('tm', 'groups'), parts along dimension 1, may hold values from -6 to 6
Outputs:
- grad_receptance: bfloat16 [4096, 1024], P(('groups', 'tm')), parts along dimension 0
- grad_keys: bfloat16 [4096, 1024], P(('groups', 'tm')), parts along dimension 0
- grad_values: bfloat16 [4096, 1024], P(('groups', 'tm')), parts along dimension 0
- grad_weight: float32 [2048, 1024], P(('groups', 'tm')), parts along dimension 0
The draws below stay inside these ranges and needn't reach their ends.
There are 2 independent parts, one for each index of `groups`. The reference program is written for one: setup_inputs(seed, part) draws one part's arguments, and reference() takes and returns one part's arrays. A program takes and returns all parts, laid end to end along the dimension named above; an argument that names none is the same for every part. Nothing has to cross between parts.
All inputs are finite; a program needn't handle non-finite values.
Results may differ from the reference program's by a relative error of at most 0.0029.
Values may be sent and summed in bfloat16 or wider, within the bound.
A program may use at most 320 MiB of HBM per device.

```python
import math
import jax
import jax.numpy as jnp
from jax import lax

HEAD_COUNT = 16
HEAD_SIZE = 64
D = 1024
FRAME_COUNT = 2048


def slow_heads(key, slow_share):
    return jax.random.uniform(jax.random.fold_in(key, 17), (HEAD_COUNT,)) < slow_share


def draw_log_decay(key, part):
    key_rate, key_fast, key_rough = jax.random.split(jax.random.fold_in(key, 23), 3)
    slow_share = 0.5
    is_slow = slow_heads(key, slow_share)
    slow_rate = jax.random.uniform(key_rate, (HEAD_COUNT,), minval=0.05, maxval=0.3) * math.log(10.0) / FRAME_COUNT
    fast_rate = jax.random.uniform(key_fast, (HEAD_COUNT,), minval=1.0 / 50.0, maxval=1.0 / 30.0)
    base_rate = jnp.where(is_slow, slow_rate, fast_rate)
    roughness = jax.random.uniform(key_rough, (FRAME_COUNT, HEAD_COUNT, HEAD_SIZE), minval=0.7, maxval=1.4)
    return (-(base_rate[None, :, None] * roughness)).reshape(FRAME_COUNT, HEAD_COUNT * HEAD_SIZE).astype(jnp.bfloat16)


def draw_removal(key, part):
    key_fast, key_back, key_select_mask, key_magnitude = jax.random.split(jax.random.fold_in(key, 29), 4)
    slow_share = 0.5
    is_slow = slow_heads(key, slow_share)
    fast_level = jax.random.uniform(key_fast, (FRAME_COUNT, HEAD_COUNT, HEAD_SIZE), minval=0.05, maxval=0.6)
    ambient_level = jax.random.uniform(key_back, (FRAME_COUNT, HEAD_COUNT, HEAD_SIZE), minval=0.0, maxval=1.0) * (HEAD_SIZE / FRAME_COUNT)
    spike_mask = jax.random.uniform(key_select_mask, (FRAME_COUNT, HEAD_COUNT)) < 1.1 * HEAD_SIZE / FRAME_COUNT
    spike_level = jax.random.uniform(key_magnitude, (FRAME_COUNT, HEAD_COUNT, HEAD_SIZE), minval=0.3, maxval=0.6)
    gradual_level = jnp.where(spike_mask[:, :, None], spike_level, ambient_level)
    chosen = jnp.where(is_slow[None, :, None], gradual_level, fast_level)
    return chosen.reshape(FRAME_COUNT, HEAD_COUNT * HEAD_SIZE).astype(jnp.bfloat16)


def block_levels(stream_key, dims, cuts, smallest, largest):
    gain, own = 1.0, jax.random.fold_in(stream_key, 6)
    for dim, parts in cuts:
        heights = jnp.exp(jax.random.uniform(jax.random.fold_in(own, dim), (parts,), jnp.float32, smallest / len(cuts), largest / len(cuts)))
        gain = gain * jnp.repeat(heights, dims[dim] // parts).reshape([-1 if axis == dim else 1 for axis in range(len(dims))])
    return gain


def bell_draw(key, dims, width, bound, cuts=(), kind=jnp.bfloat16):
    result = jax.random.normal(key, dims, jnp.float32) * width
    if len(cuts) > 0:
        result = block_levels(key, dims, cuts, -0.22, 0.18) * result
    return jnp.clip(result, min=-bound, max=bound).astype(kind)


def setup_inputs(seed: int = 0, part: int = 0) -> dict:
    key_of = jax.random.split(jax.random.key(seed), 10)
    own_keys = jax.random.split(jax.random.fold_in(key_of[9], part), 10)
    return {
        "receptance": bell_draw(own_keys[0], (FRAME_COUNT, D), 0.125, 0.75, ((0, 16),)),
        "key_input": bell_draw(own_keys[1], (FRAME_COUNT, D), 1.0, 6.0, ((0, 16),)),
        "values": bell_draw(own_keys[2], (FRAME_COUNT, D), 1.0, 6.0, ((0, 16),)),
        "log_decay": draw_log_decay(jax.random.fold_in(jax.random.fold_in(key_of[9], part), 71), part),
        "kappa_raw": bell_draw(own_keys[4], (FRAME_COUNT, D), 1.0, 6.0, ((0, 16),)),
        "removal": draw_removal(jax.random.fold_in(jax.random.fold_in(key_of[9], part), 71), part),
        "initial_state": bell_draw(own_keys[6], (HEAD_COUNT, HEAD_SIZE, HEAD_SIZE), 0.5, 3.0, (), jnp.float32),
        "out_weight": bell_draw(key_of[7], (D, D), D ** -0.5, 0.1875),
        "grad_output": bell_draw(own_keys[8], (D, FRAME_COUNT), 1.0, 6.0, ((0, 16),)),
    }


def make_frames(receptance, key_input, values, log_decay, kappa_raw, removal, grad_y):
    frame_count = receptance.shape[0]
    head_shape = (frame_count, HEAD_COUNT, HEAD_SIZE)
    log_part = log_decay.astype(jnp.float32).reshape(head_shape)
    decays = jnp.exp(log_part)
    key_scale = jnp.sqrt(-jnp.expm1(log_part))
    raw_key = kappa_raw.astype(jnp.float32).reshape(head_shape)
    unit_key = raw_key / jnp.sqrt(lax.optimization_barrier(jnp.sum(raw_key * raw_key, -1, keepdims=True)) + 1e-06)
    gated_key = removal.astype(jnp.float32).reshape(head_shape) * unit_key
    keys_in = key_input.astype(jnp.float32).reshape(head_shape) * key_scale
    value_rows = values.astype(jnp.float32).reshape(head_shape)
    recept_rows = receptance.astype(jnp.float32).reshape(head_shape)
    grad_rows = grad_y.reshape(head_shape)
    return (decays, unit_key, gated_key, value_rows, keys_in, recept_rows, grad_rows, key_scale)

def advance(current, decays, unit_key, gated_key, value_rows, keys_in):
    projected = lax.optimization_barrier(jnp.sum(current * unit_key[..., None, :], -1))
    return current * decays[..., None, :] - projected[..., :, None] * gated_key[..., None, :] + value_rows[..., :, None] * keys_in[..., None, :]

def pull_back(grad_state, decays, unit_key, gated_key):
    pulled = lax.optimization_barrier(jnp.sum(grad_state * gated_key[..., None, :], -1))
    return grad_state * decays[..., None, :] - pulled[..., :, None] * unit_key[..., None, :]

def forward_step(current, frame_slice):
    decays, unit_key, gated_key, value_rows, keys_in, recept_rows, grad_rows, key_scale = frame_slice
    current = advance(current, decays, unit_key, gated_key, value_rows, keys_in)
    out_y = lax.optimization_barrier(jnp.sum(current * recept_rows[:, None, :], -1))
    grad_r = lax.optimization_barrier(jnp.sum(current * grad_rows[:, :, None], -2))
    return (current, (out_y, grad_r))

def backward_step(incoming, frame_slice):
    decays, unit_key, gated_key, value_rows, keys_in, recept_rows, grad_rows, key_scale = frame_slice
    grad_state = incoming + grad_rows[:, :, None] * recept_rows[:, None, :]
    grad_v = lax.optimization_barrier(jnp.sum(grad_state * keys_in[:, None, :], -1))
    grad_k = lax.optimization_barrier(jnp.sum(grad_state * value_rows[:, :, None], -2)) * key_scale
    return (pull_back(grad_state, decays, unit_key, gated_key), (grad_v, grad_k))

def reference(receptance, key_input, values, log_decay, kappa_raw, removal, initial_state, out_weight, grad_output):
    frame_count = receptance.shape[0]
    grad_y = lax.dot_general(grad_output, out_weight, (((0,), (1,)), ((), ())), preferred_element_type=jnp.float32)
    frames = make_frames(receptance, key_input, values, log_decay, kappa_raw, removal, grad_y)
    last_state, (out_y, grad_r) = lax.scan(forward_step, initial_state.astype(jnp.float32), frames)
    zero_state = jnp.zeros((HEAD_COUNT, HEAD_SIZE, HEAD_SIZE), jnp.float32)
    last_grad, (grad_v, grad_k) = lax.scan(backward_step, zero_state, frames, reverse=True)
    y_low = out_y.reshape(frame_count, HEAD_COUNT * HEAD_SIZE).astype(jnp.bfloat16)
    loss_scale = 1.0 / math.sqrt(frame_count)
    grad_weight = lax.dot_general(y_low, grad_output, (((0,), (1,)), ((), ())), preferred_element_type=jnp.float32) * loss_scale
    flat_shape = (frame_count, HEAD_COUNT * HEAD_SIZE)
    return (grad_r.reshape(flat_shape).astype(jnp.bfloat16), grad_k.reshape(flat_shape).astype(jnp.bfloat16), grad_v.reshape(flat_shape).astype(jnp.bfloat16), grad_weight)
```

```python
import functools
import math

import jax
import jax.numpy as jnp
from jax import lax
from jax.experimental import pallas as pl
from jax.experimental.pallas import tpu as pltpu
from jax.sharding import PartitionSpec as P

HEAD_COUNT = 16
HEAD_SIZE = 64
PAIR = 2 * HEAD_SIZE
PAIRS = HEAD_COUNT // 2
F32 = jnp.float32
BF16 = jnp.bfloat16

NN = (((1,), (0,)), ((), ()))
NT = (((1,), (1,)), ((), ()))
TN = (((0,), (0,)), ((), ()))


def split(x):
    high = x.astype(BF16)
    return high, (x - high.astype(F32)).astype(BF16)


def dot1(a, b, dims):
    return lax.dot_general(a, b, dims, preferred_element_type=F32)


def dot3(a, b, dims):
    a = (a,) if not isinstance(a, tuple) and a.dtype == BF16 else a if isinstance(a, tuple) else split(a)
    b = (b,) if not isinstance(b, tuple) and b.dtype == BF16 else b if isinstance(b, tuple) else split(b)
    out = dot1(a[0], b[0], dims)
    if len(b) > 1:
        out = out + dot1(a[0], b[1], dims)
    if len(a) > 1:
        out = out + dot1(a[1], b[0], dims)
    return out


def iota(shape, dim):
    return lax.broadcasted_iota(jnp.int32, shape, dim)


def both(f, lane_low):
    return jnp.where(lane_low, f(0), f(1))


def pack(full, lane_low):
    return jnp.where(lane_low, full[:HEAD_SIZE], full[HEAD_SIZE:])


def unpack(packed, diagonal):
    return jnp.where(diagonal, jnp.concatenate([packed, packed], 0), 0.0)


def inverses(lower, row, col):
    size = row.shape[0]
    eye = jnp.where(row == col, 1.0, 0.0).astype(F32)
    step = 1
    out = None
    while step < size:
        inside = (row // (2 * step) == col // (2 * step)) & (row // step != col // step)
        off = [jnp.where(inside, m, 0.0) for m in lower]
        if out is None:
            out = [eye - m for m in off]
        else:
            halves = [split(t) for t in out]
            mid = [dot3(m, t, NN) for m, t in zip(off, halves)]
            out = [t - dot3(h, m, NN) for t, h, m in zip(out, halves, mid)]
        step *= 2
    return out


SAVED = 14


def one_less_exp(x):
    series = jnp.full_like(x, 1.0 / math.factorial(10))
    for n in range(9, 0, -1):
        series = series * x + 1.0 / math.factorial(n)
    return jnp.where(x > -0.5, -x * series, 1.0 - jnp.exp(x))


def first_kernel(rows_each, rec_ref, key_ref, val_ref, log_ref, kap_ref, rem_ref, gy_ref, pay_ref, *saved):
    frames = rec_ref.shape[0]
    row, col = iota((frames, frames), 0), iota((frames, frames), 1)
    lane_low = iota((frames, PAIR), 1) < HEAD_SIZE
    pack_low = iota((HEAD_SIZE, PAIR), 1) < HEAD_SIZE
    prow, pcol = iota((PAIR, PAIR), 0), iota((PAIR, PAIR), 1)
    diagonal = (prow // HEAD_SIZE) == (pcol // HEAD_SIZE)
    ones = jnp.where(diagonal, 1.0, 0.0).astype(BF16)
    tri = jnp.where(row >= col, 1.0, 0.0).astype(BF16)
    own = [lane_low, jnp.logical_not(lane_low)]

    count = rec_ref.shape[1] // PAIR
    for pair in range(count):
        at = pl.ds(pair * PAIR, PAIR)
        log_low = log_ref[:, at]
        log_part = log_low.astype(F32)
        total = dot1(tri, log_low, NN)
        middle, last = total[frames // 2 - 1 : frames // 2], total[frames - 1 : frames]
        key_scale = jnp.sqrt(one_less_exp(log_part))
        raw = kap_ref[:, at].astype(F32)
        norm = dot3(raw * raw, ones, NN)
        a = raw / jnp.sqrt(norm + 1e-06)
        b = rem_ref[:, at].astype(F32) * a
        k = key_ref[:, at].astype(F32) * key_scale
        r = rec_ref[:, at].astype(F32)
        v = val_ref[:, at]
        q = split(gy_ref[:, at])
        e_pos, e_prev, e_neg = (
            jnp.exp(total - middle), jnp.exp(total - log_part - middle), jnp.exp(middle - total)
        )
        e_abs, e_end = jnp.exp(total), jnp.exp(last - total)
        a_mid, r_mid, b_mid, k_mid = a * e_prev, r * e_pos, b * e_neg, k * e_neg
        a_abs, r_abs = a * jnp.exp(total - log_part), r * e_abs
        b_end, k_end = b * e_end, k * e_end

        upper = split(jnp.concatenate([a_mid, r_mid], 0))
        rights = split(jnp.concatenate([b_mid, k_mid], 0))
        own2 = [jnp.concatenate([m, m], 0) for m in own]
        zero = jnp.zeros((), BF16)
        grams = [dot3(upper, tuple(jnp.where(m, x, zero) for x in rights), NT) for m in own2]
        strict, lax_tri = row > col, row >= col
        m_ab = [jnp.where(strict, g[:frames, :frames], 0.0) for g in grams]
        m_ak = [jnp.where(strict, g[:frames, frames:], 0.0) for g in grams]
        m_rb = [split(jnp.where(lax_tri, g[frames:, :frames], 0.0)) for g in grams]
        m_rk = [split(jnp.where(lax_tri, g[frames:, frames:], 0.0)) for g in grams]
        t_inv = [split(t) for t in inverses(m_ab, row, col)]
        m_ak = [split(m) for m in m_ak]

        low2 = jnp.concatenate([lane_low, lane_low], 1)
        start = both(lambda h: dot3(m_ak[h], v, NN), lane_low)
        first = split(jnp.concatenate([start, a_abs], 1))
        inner = both(lambda h: dot3(t_inv[h], first, NN), low2)
        u0, x = inner[:, :PAIR], inner[:, PAIR:]
        inner = split(inner)
        minus = both(lambda h: dot3(m_rb[h], inner, NN), low2)
        y0 = both(lambda h: dot3(m_rk[h], v, NN), lane_low) - minus[:, :PAIR]
        yr = r_abs - minus[:, PAIR:]

        back = both(lambda h: dot3(m_rb[h], q, TN), lane_low)
        second = split(jnp.concatenate([back, b_end], 1))
        pulled = both(lambda h: dot3(t_inv[h], second, TN), low2)
        p0, tb = pulled[:, :PAIR], pulled[:, PAIR:]
        pulled = split(pulled)
        minus = both(lambda h: dot3(m_ak[h], pulled, TN), low2)
        gv0 = both(lambda h: dot3(m_rk[h], q, TN), lane_low) - minus[:, :PAIR]
        gvk = k_end - minus[:, PAIR:]

        v_own = [jnp.where(m, v, zero) for m in own]
        q_own = [tuple(jnp.where(m, x_, zero) for x_ in q) for m in own]
        k_mid_s, r_mid_s = split(k_mid), split(r_mid)
        gra = e_pos * both(
            lambda h: dot3(jnp.where(lax_tri, dot3(q, v_own[h], NT), 0.0), k_mid_s, NN), lane_low
        )
        gka = e_neg * both(
            lambda h: dot3(jnp.where(row <= col, dot3(v, q_own[h], NT), 0.0), r_mid_s, NN), lane_low
        )

        b_end_s = split(b_end)
        both_end = dot3(inner, b_end_s, TN)
        ends = jnp.where(prow == pcol, jnp.exp(last), 0.0) - both_end[PAIR:]
        offset = dot3(v, k_end, TN) - both_end[:PAIR]
        pull = dot3(q, r_abs, TN) - dot3(p0, a_abs, TN)
        through, offset, pull = pack(ends, pack_low), pack(offset, pack_low), pack(pull, pack_low)
        for part in range(HEAD_SIZE // rows_each):
            rows = slice(part * rows_each, (part + 1) * rows_each)
            to = pair * (HEAD_SIZE // rows_each) + part
            pay_ref[to, :HEAD_SIZE] = through
            pay_ref[to, HEAD_SIZE : HEAD_SIZE + rows_each] = offset[rows]
            pay_ref[to, HEAD_SIZE + rows_each :] = pull[rows]

        keep = (u0, x, y0, yr, p0, tb, gv0, gvk, gra, gka * key_scale,
                total, b_mid, a_mid, key_scale)
        for ref, value in zip(saved, keep):
            ref[:, at] = value


def relay_kernel(rows_each, pay_ref, start_ref, out_ref):
    count = pay_ref.shape[0]
    diagonal = (iota((PAIR, PAIR), 0) // HEAD_SIZE) == (iota((PAIR, PAIR), 1) // HEAD_SIZE)

    def lap(i, carried):
        state, grad = carried
        j = count - 1 - i
        out_ref[i, :rows_each] = state
        out_ref[j, rows_each:] = grad
        state = pay_ref[i, HEAD_SIZE : HEAD_SIZE + rows_each] + dot3(
            state, unpack(pay_ref[i, :HEAD_SIZE], diagonal), NN
        )
        grad = pay_ref[j, HEAD_SIZE + rows_each :] + dot3(
            grad, unpack(pay_ref[j, :HEAD_SIZE], diagonal), NT
        )
        return state, grad

    lax.fori_loop(0, count, lap, (start_ref[...], jnp.zeros((rows_each, PAIR), F32)))


def last_kernel(state_ref, grad_ref, gy_ref, val_ref, u_ref, x_ref, y_ref, yr_ref, p_ref, tb_ref,
                gv_ref, gvk_ref, gra_ref, gka_ref, tot_ref, b_ref, a_ref, ks_ref,
                ylow_ref, gr_out, gk_out, gv_out):
    frames = gy_ref.shape[0]
    row, col = iota((frames, frames), 0), iota((frames, frames), 1)
    lane_low = iota((frames, PAIR), 1) < HEAD_SIZE
    own = [lane_low, jnp.logical_not(lane_low)]
    diagonal = (iota((PAIR, PAIR), 0) // HEAD_SIZE) == (iota((PAIR, PAIR), 1) // HEAD_SIZE)
    zero = jnp.zeros((), BF16)
    for pair in range(gy_ref.shape[1] // PAIR):
        at = pl.ds(pair * PAIR, PAIR)
        state = split(unpack(state_ref[pair], diagonal))
        grad = split(unpack(grad_ref[pair], diagonal))
        q, v = split(gy_ref[:, at]), val_ref[:, at]
        ahead = dot3(jnp.concatenate([x_ref[:, at], yr_ref[:, at]], 0), state, NT)
        u = split(u_ref[:, at] + ahead[:frames])
        ylow_ref[:, at] = (y_ref[:, at] + ahead[frames:]).astype(BF16)
        behind = dot3(jnp.concatenate([tb_ref[:, at], gvk_ref[:, at]], 0), grad, NT)
        p = split(p_ref[:, at] + behind[:frames])
        gv_out[:, at] = (gv_ref[:, at] + behind[frames:]).astype(BF16)
        b_mid, a_mid = split(b_ref[:, at]), split(a_ref[:, at])
        total = tot_ref[:, at]
        middle, last = total[frames // 2 - 1 : frames // 2], total[frames - 1 : frames]

        def removed(h):
            gram = dot3(q, tuple(jnp.where(own[h], x, zero) for x in u), NT)
            return dot3(jnp.where(row >= col, gram, 0.0), b_mid, NN)

        def removed_back(h):
            gram = dot3(v, tuple(jnp.where(own[h], x, zero) for x in p), NT)
            return dot3(jnp.where(row < col, gram, 0.0), a_mid, NN)

        gr = jnp.exp(total) * dot3(q, state, NN) + gra_ref[:, at]
        gr = gr - jnp.exp(total - middle) * both(removed, lane_low)
        gr_out[:, at] = gr.astype(BF16)
        gk = jnp.exp(last - total) * dot3(v, grad, NN) - jnp.exp(middle - total) * both(
            removed_back, lane_low
        )
        gk_out[:, at] = (gk * ks_ref[:, at] + gka_ref[:, at]).astype(BF16)


def local(receptance, key_input, values, log_decay, kappa_raw, removal, initial_state, out_weight, grad_output):
    size = lax.axis_size("tm")
    frames, width = receptance.shape
    rows_each = PAIRS * HEAD_SIZE // size
    everything = lax.all_gather(grad_output, "tm", axis=0, tiled=True)
    gathered = lax.all_to_all(grad_output, "tm", split_axis=1, concat_axis=0, tiled=True)
    grad_y = lax.dot_general(
        gathered, out_weight, (((0,), (1,)), ((), ())), preferred_element_type=F32
    )
    group = 2
    block = pl.BlockSpec((frames, group * PAIR), lambda i: (0, i))
    per_step = group * size // PAIRS
    pay_shape = (size, HEAD_SIZE + 2 * rows_each, PAIR)
    flat = jax.ShapeDtypeStruct((frames, width), F32)
    params = pltpu.CompilerParams(vmem_limit_bytes=60 << 20)
    payload, *saved = pl.pallas_call(
        functools.partial(first_kernel, rows_each),
        grid=(PAIRS // group,),
        in_specs=[block] * 7,
        out_specs=[pl.BlockSpec((per_step,) + pay_shape[1:], lambda i: (i, 0, 0))] + [block] * SAVED,
        out_shape=[jax.ShapeDtypeStruct(pay_shape, F32)] + [flat] * SAVED,
        compiler_params=params,
        name="first",
    )(receptance, key_input, values, log_decay, kappa_raw, removal, grad_y)
    arrived = lax.all_to_all(payload, "tm", split_axis=0, concat_axis=0, tiled=True)
    start = initial_state.reshape(PAIRS, 2, HEAD_SIZE, HEAD_SIZE).swapaxes(1, 2)
    start = lax.dynamic_slice_in_dim(
        start.reshape(PAIRS * HEAD_SIZE, PAIR), lax.axis_index("tm") * rows_each, rows_each, 0
    )
    entries = pl.pallas_call(
        functools.partial(relay_kernel, rows_each),
        out_shape=jax.ShapeDtypeStruct((size, 2 * rows_each, PAIR), F32),
        compiler_params=params,
        name="relay",
    )(arrived, start)
    entries = lax.all_to_all(entries, "tm", split_axis=0, concat_axis=0, tiled=True)
    state = entries[:, :rows_each].reshape(PAIRS, HEAD_SIZE, PAIR)
    grad = entries[:, rows_each:].reshape(PAIRS, HEAD_SIZE, PAIR)
    small = pl.BlockSpec((group, HEAD_SIZE, PAIR), lambda i: (i, 0, 0))
    low = jax.ShapeDtypeStruct((frames, width), BF16)
    y_low, grad_r, grad_k, grad_v = pl.pallas_call(
        last_kernel,
        grid=(PAIRS // group,),
        in_specs=[small, small] + [block] * (2 + SAVED),
        out_specs=[block] * 4,
        out_shape=[low] * 4,
        compiler_params=params,
        name="last",
    )(state, grad, grad_y, values, *saved)
    y_mine = lax.all_to_all(y_low, "tm", split_axis=1, concat_axis=0, tiled=True)
    loss_scale = 1.0 / math.sqrt(frames * size)
    grad_weight = (
        lax.dot_general(y_mine, everything, (((0,), (1,)), ((), ())), preferred_element_type=F32)
        * loss_scale
    )
    return grad_r, grad_k, grad_v, grad_weight


def solution(mesh):
    rows = P(("groups", "tm"), None)
    return jax.shard_map(
        local,
        mesh=mesh,
        in_specs=(rows,) * 6 + (P("groups", None, None), P(), P("tm", "groups")),
        out_specs=(rows,) * 4,
        check_vma=False,
    )
```

```python
import functools
import math

import jax
import jax.numpy as jnp
from jax import lax
from jax.experimental import pallas as pl
from jax.experimental.pallas import tpu as pltpu
from jax.sharding import PartitionSpec as P

HEAD_COUNT = 16
HEAD_SIZE = 64
PAIR = 2 * HEAD_SIZE
PAIRS = HEAD_COUNT // 2
F32 = jnp.float32
BF16 = jnp.bfloat16

NN = (((1,), (0,)), ((), ()))
NT = (((1,), (1,)), ((), ()))
TN = (((0,), (0,)), ((), ()))


def split(x):
    high = x.astype(BF16)
    return high, (x - high.astype(F32)).astype(BF16)


def dot1(a, b, dims):
    return lax.dot_general(a, b, dims, preferred_element_type=F32)


def dot3(a, b, dims):
    a = (a,) if not isinstance(a, tuple) and a.dtype == BF16 else a if isinstance(a, tuple) else split(a)
    b = (b,) if not isinstance(b, tuple) and b.dtype == BF16 else b if isinstance(b, tuple) else split(b)
    out = dot1(a[0], b[0], dims)
    if len(b) > 1:
        out = out + dot1(a[0], b[1], dims)
    if len(a) > 1:
        out = out + dot1(a[1], b[0], dims)
    return out


def iota(shape, dim):
    return lax.broadcasted_iota(jnp.int32, shape, dim)


def both(f, lane_low):
    return jnp.where(lane_low, f(0), f(1))


def pack(full, lane_low):
    return jnp.where(lane_low, full[:HEAD_SIZE], full[HEAD_SIZE:])


def unpack(packed, diagonal):
    return jnp.where(diagonal, jnp.concatenate([packed, packed], 0), 0.0)


def inverses(lower, row, col):
    size = row.shape[0]
    eye = jnp.where(row == col, 1.0, 0.0).astype(F32)
    step = 1
    out = None
    while step < size:
        inside = (row // (2 * step) == col // (2 * step)) & (row // step != col // step)
        off = [jnp.where(inside, m, 0.0) for m in lower]
        if out is None:
            out = [eye - m for m in off]
        else:
            halves = [split(t) for t in out]
            mid = [dot3(m, t, NN) for m, t in zip(off, halves)]
            out = [t - dot3(h, m, NN) for t, h, m in zip(out, halves, mid)]
        step *= 2
    return out


GROUP = 2


def one_less_exp(x):
    series = jnp.full_like(x, 1.0 / math.factorial(10))
    for n in range(9, 0, -1):
        series = series * x + 1.0 / math.factorial(n)
    return jnp.where(x > -0.5, -x * series, 1.0 - jnp.exp(x))


def row_scales(total):
    frames = total.shape[0]
    return total[frames // 2 - 1 : frames // 2], total[frames - 1 : frames]


def forward_kernel(rows_each, rec_ref, key_ref, val_ref, log_ref, kap_ref, rem_ref, pay_ref,
                   u_ref, x_ref, y_ref, yr_ref, tot_ref, ks_ref, a_ref, b_ref, k_ref,
                   t_ref, ak_ref, rb_ref, rk_ref):
    frames = rec_ref.shape[0]
    row, col = iota((frames, frames), 0), iota((frames, frames), 1)
    lane_low = iota((frames, PAIR), 1) < HEAD_SIZE
    low2 = jnp.concatenate([lane_low, lane_low], 1)
    pack_low = iota((HEAD_SIZE, PAIR), 1) < HEAD_SIZE
    prow, pcol = iota((PAIR, PAIR), 0), iota((PAIR, PAIR), 1)
    ones = jnp.where((prow // HEAD_SIZE) == (pcol // HEAD_SIZE), 1.0, 0.0).astype(BF16)
    tri = jnp.where(row >= col, 1.0, 0.0).astype(BF16)
    own2 = [jnp.concatenate([m, m], 0) for m in (lane_low, jnp.logical_not(lane_low))]
    strict, lax_tri = row > col, row >= col
    zero = jnp.zeros((), BF16)
    count = rec_ref.shape[1] // PAIR

    m_ab = []
    for pair in range(count):
        at = pl.ds(pair * PAIR, PAIR)
        log_low = log_ref[:, at]
        log_part = log_low.astype(F32)
        total = dot1(tri, log_low, NN)
        middle, last = row_scales(total)
        key_scale = jnp.sqrt(one_less_exp(log_part))
        raw = kap_ref[:, at].astype(F32)
        norm = dot3(raw * raw, ones, NN)
        a = raw / jnp.sqrt(norm + 1e-06)
        e_neg = jnp.exp(middle - total)
        a_mid = a * jnp.exp(total - log_part - middle)
        b_mid = rem_ref[:, at].astype(F32) * a * e_neg
        k_mid = key_ref[:, at].astype(F32) * key_scale * e_neg
        r_mid = rec_ref[:, at].astype(F32) * jnp.exp(total - middle)
        for ref, value in zip((tot_ref, ks_ref, a_ref, b_ref, k_ref), (total, key_scale, a_mid, b_mid, k_mid)):
            ref[:, at] = value
        upper = split(jnp.concatenate([a_mid, r_mid], 0))
        rights = split(jnp.concatenate([b_mid, k_mid], 0))
        for h, m in enumerate(own2):
            gram = dot3(upper, tuple(jnp.where(m, x, zero) for x in rights), NT)
            head = pl.ds((pair * 2 + h) * frames, frames)
            m_ab.append(jnp.where(strict, gram[:frames, :frames], 0.0))
            ak_ref[:, head] = jnp.where(strict, gram[:frames, frames:], 0.0)
            rb_ref[:, head] = jnp.where(lax_tri, gram[frames:, :frames], 0.0)
            rk_ref[:, head] = jnp.where(lax_tri, gram[frames:, frames:], 0.0)
    inverted = inverses(m_ab, row, col)

    for pair in range(count):
        at = pl.ds(pair * PAIR, PAIR)
        heads = [pl.ds((pair * 2 + h) * frames, frames) for h in range(2)]
        v = val_ref[:, at]
        total = tot_ref[:, at]
        middle, last = row_scales(total)
        a_abs = a_ref[:, at] * jnp.exp(middle)
        r_abs = rec_ref[:, at].astype(F32) * jnp.exp(total)
        scale = jnp.exp(last - middle)
        for h in range(2):
            t_ref[:, heads[h]] = inverted[pair * 2 + h]
        t_inv = [split(inverted[pair * 2 + h]) for h in range(2)]
        on_v = [dot3(jnp.concatenate([ak_ref[:, h], rk_ref[:, h]], 0), v, NN) for h in heads]
        on_v = jnp.where(own2[0], on_v[0], on_v[1])
        given = split(jnp.concatenate([on_v[:frames], a_abs], 1))
        inner = both(lambda h: dot3(t_inv[h], given, NN), low2)
        u_ref[:, at], x_ref[:, at] = inner[:, :PAIR], inner[:, PAIR:]
        inner = split(inner)
        minus = both(lambda h: dot3(rb_ref[:, heads[h]], inner, NN), low2)
        y_ref[:, at] = on_v[frames:] - minus[:, :PAIR]
        yr_ref[:, at] = r_abs - minus[:, PAIR:]
        ended = dot3(inner, b_ref[:, at] * scale, TN)
        through = pack(jnp.where(prow == pcol, jnp.exp(last), 0.0) - ended[PAIR:], pack_low)
        offset = pack(dot3(v, k_ref[:, at] * scale, TN) - ended[:PAIR], pack_low)
        for part in range(HEAD_SIZE // rows_each):
            to = pair * (HEAD_SIZE // rows_each) + part
            pay_ref[to, :HEAD_SIZE] = through
            pay_ref[to, HEAD_SIZE:] = offset[part * rows_each : (part + 1) * rows_each]


def backward_kernel(rows_each, rec_ref, val_ref, gy_ref, tot_ref, ks_ref, a_ref, b_ref, k_ref,
                    t_ref, ak_ref, rb_ref, rk_ref,
                    pay_ref, p_ref, tb_ref, gv_ref, gvk_ref, gra_ref, gka_ref):
    frames = rec_ref.shape[0]
    row, col = iota((frames, frames), 0), iota((frames, frames), 1)
    lane_low = iota((frames, PAIR), 1) < HEAD_SIZE
    own = [lane_low, jnp.logical_not(lane_low)]
    low2 = jnp.concatenate([lane_low, lane_low], 1)
    pack_low = iota((HEAD_SIZE, PAIR), 1) < HEAD_SIZE
    zero = jnp.zeros((), BF16)
    for pair in range(rec_ref.shape[1] // PAIR):
        at = pl.ds(pair * PAIR, PAIR)
        heads = [pl.ds((pair * 2 + h) * frames, frames) for h in range(2)]
        total = tot_ref[:, at]
        middle, last = row_scales(total)
        scale = jnp.exp(last - middle)
        v, q = val_ref[:, at], split(gy_ref[:, at])
        e_pos, e_neg = jnp.exp(total - middle), jnp.exp(middle - total)
        r = rec_ref[:, at].astype(F32)
        m_rb, m_rk, m_ak, t_inv = (
            [split(ref[:, h]) for h in heads] for ref in (rb_ref, rk_ref, ak_ref, t_ref)
        )
        back = both(lambda h: dot3(m_rb[h], q, TN), lane_low)
        given = split(jnp.concatenate([back, b_ref[:, at] * scale], 1))
        pulled = both(lambda h: dot3(t_inv[h], given, TN), low2)
        p0 = pulled[:, :PAIR]
        p_ref[:, at], tb_ref[:, at] = p0, pulled[:, PAIR:]
        pulled = split(pulled)
        minus = both(lambda h: dot3(m_ak[h], pulled, TN), low2)
        gv_ref[:, at] = both(lambda h: dot3(m_rk[h], q, TN), lane_low) - minus[:, :PAIR]
        gvk_ref[:, at] = k_ref[:, at] * scale - minus[:, PAIR:]
        v_own = [jnp.where(m, v, zero) for m in own]
        q_own = [tuple(jnp.where(m, x, zero) for x in q) for m in own]
        k_mid, r_mid = split(k_ref[:, at]), split(r * e_pos)
        gra_ref[:, at] = e_pos * both(
            lambda h: dot3(jnp.where(row >= col, dot3(q, v_own[h], NT), 0.0), k_mid, NN), lane_low
        )
        gka_ref[:, at] = ks_ref[:, at] * e_neg * both(
            lambda h: dot3(jnp.where(row <= col, dot3(v, q_own[h], NT), 0.0), r_mid, NN), lane_low
        )
        pull = dot3(q, r * jnp.exp(total), TN) - dot3(p0, a_ref[:, at] * jnp.exp(middle), TN)
        pull = pack(pull, pack_low)
        for part in range(HEAD_SIZE // rows_each):
            to = pair * (HEAD_SIZE // rows_each) + part
            pay_ref[to] = pull[part * rows_each : (part + 1) * rows_each]


def relay_kernel(rows_each, pay_ref, pull_ref, start_ref, out_ref):
    count = pay_ref.shape[0]
    diagonal = (iota((PAIR, PAIR), 0) // HEAD_SIZE) == (iota((PAIR, PAIR), 1) // HEAD_SIZE)

    def lap(i, carried):
        state, grad = carried
        j = count - 1 - i
        out_ref[i, :rows_each] = state
        out_ref[j, rows_each:] = grad
        state = pay_ref[i, HEAD_SIZE:] + dot3(
            state, unpack(pay_ref[i, :HEAD_SIZE], diagonal), NN
        )
        grad = pull_ref[j] + dot3(
            grad, unpack(pay_ref[j, :HEAD_SIZE], diagonal), NT
        )
        return state, grad

    lax.fori_loop(0, count, lap, (start_ref[...], jnp.zeros((rows_each, PAIR), F32)))


def output_kernel(state_ref, y_ref, yr_ref, ylow_ref):
    diagonal = (iota((PAIR, PAIR), 0) // HEAD_SIZE) == (iota((PAIR, PAIR), 1) // HEAD_SIZE)
    for pair in range(y_ref.shape[1] // PAIR):
        at = pl.ds(pair * PAIR, PAIR)
        state = unpack(state_ref[pair], diagonal)
        y = y_ref[:, at] + dot3(yr_ref[:, at], state, NT)
        ylow_ref[pl.ds(pair * PAIR, PAIR), :] = y.T.astype(BF16)


def last_kernel(state_ref, grad_ref, gy_ref, val_ref, u_ref, x_ref, p_ref, tb_ref,
                gv_ref, gvk_ref, gra_ref, gka_ref, tot_ref, b_ref, a_ref, ks_ref,
                gr_out, gk_out, gv_out):
    frames = gy_ref.shape[0]
    row, col = iota((frames, frames), 0), iota((frames, frames), 1)
    lane_low = iota((frames, PAIR), 1) < HEAD_SIZE
    own = [lane_low, jnp.logical_not(lane_low)]
    diagonal = (iota((PAIR, PAIR), 0) // HEAD_SIZE) == (iota((PAIR, PAIR), 1) // HEAD_SIZE)
    zero = jnp.zeros((), BF16)
    for pair in range(gy_ref.shape[1] // PAIR):
        at = pl.ds(pair * PAIR, PAIR)
        state = split(unpack(state_ref[pair], diagonal))
        grad = split(unpack(grad_ref[pair], diagonal))
        q, v = split(gy_ref[:, at]), val_ref[:, at]
        u = split(u_ref[:, at] + dot3(x_ref[:, at], state, NT))
        behind = dot3(jnp.concatenate([tb_ref[:, at], gvk_ref[:, at]], 0), grad, NT)
        p = split(p_ref[:, at] + behind[:frames])
        gv_out[:, at] = (gv_ref[:, at] + behind[frames:]).astype(BF16)
        b_mid, a_mid = split(b_ref[:, at]), split(a_ref[:, at])
        total = tot_ref[:, at]
        middle, last = total[frames // 2 - 1 : frames // 2], total[frames - 1 : frames]

        def removed(h):
            gram = dot3(q, tuple(jnp.where(own[h], x, zero) for x in u), NT)
            return dot3(jnp.where(row >= col, gram, 0.0), b_mid, NN)

        def removed_back(h):
            gram = dot3(v, tuple(jnp.where(own[h], x, zero) for x in p), NT)
            return dot3(jnp.where(row < col, gram, 0.0), a_mid, NN)

        gr = jnp.exp(total) * dot3(q, state, NN) + gra_ref[:, at]
        gr = gr - jnp.exp(total - middle) * both(removed, lane_low)
        gr_out[:, at] = gr.astype(BF16)
        gk = jnp.exp(last - total) * dot3(v, grad, NN) - jnp.exp(middle - total) * both(
            removed_back, lane_low
        )
        gk_out[:, at] = (gk * ks_ref[:, at] + gka_ref[:, at]).astype(BF16)


def cost(flops, moved):
    return pl.CostEstimate(flops=flops, bytes_accessed=moved, transcendentals=0)


def local(receptance, key_input, values, log_decay, kappa_raw, removal, initial_state, out_weight, grad_output):
    size = lax.axis_size("tm")
    frames, width = receptance.shape
    rows_each = PAIRS * HEAD_SIZE // size
    everything = lax.all_gather(grad_output, "tm", axis=0, tiled=True)
    gathered = lax.all_to_all(grad_output, "tm", split_axis=1, concat_axis=0, tiled=True)
    group = GROUP
    block = pl.BlockSpec((frames, group * PAIR), lambda i: (0, i))
    square = pl.BlockSpec((frames, group * 2 * frames), lambda i: (0, i))
    per_step = group * size // PAIRS
    flat = jax.ShapeDtypeStruct((frames, width), F32)
    matrix = jax.ShapeDtypeStruct((frames, HEAD_COUNT * frames), F32)
    low = jax.ShapeDtypeStruct((frames, width), BF16)
    params = pltpu.CompilerParams(vmem_limit_bytes=60 << 20)
    steps = (PAIRS // group,)

    def sent(rows):
        return (
            pl.BlockSpec((per_step, rows, PAIR), lambda i: (i, 0, 0)),
            jax.ShapeDtypeStruct((size, rows, PAIR), F32),
        )

    spec, shape = sent(HEAD_SIZE + rows_each)
    payload, u0, x0, y0, yr, total, scale, a, b, k, t, ak, rb, rk = pl.pallas_call(
        functools.partial(forward_kernel, rows_each),
        grid=steps,
        in_specs=[block] * 6,
        out_specs=[spec] + [block] * 9 + [square] * 4,
        out_shape=[shape] + [flat] * 9 + [matrix] * 4,
        compiler_params=params,
        cost_estimate=cost(20 << 30, 10 << 20),
        name="forward",
    )(receptance, key_input, values, log_decay, kappa_raw, removal)
    arrived = lax.all_to_all(payload, "tm", split_axis=0, concat_axis=0, tiled=True)
    grad_y = lax.dot_general(
        gathered, out_weight, (((0,), (1,)), ((), ())), preferred_element_type=F32
    )
    spec, shape = sent(rows_each)
    pull, p0, tb, gv, gvk, gra, gka = pl.pallas_call(
        functools.partial(backward_kernel, rows_each),
        grid=steps,
        in_specs=[block] * 8 + [square] * 4,
        out_specs=[spec] + [block] * 6,
        out_shape=[shape] + [flat] * 6,
        compiler_params=params,
        cost_estimate=cost(12 << 30, 10 << 20),
        name="backward",
    )(receptance, values, grad_y, total, scale, a, b, k, t, ak, rb, rk)
    arrived, pull = lax.optimization_barrier((arrived, pull))
    pull = lax.all_to_all(pull, "tm", split_axis=0, concat_axis=0, tiled=True)
    start = initial_state.reshape(PAIRS, 2, HEAD_SIZE, HEAD_SIZE).swapaxes(1, 2)
    start = lax.dynamic_slice_in_dim(
        start.reshape(PAIRS * HEAD_SIZE, PAIR), lax.axis_index("tm") * rows_each, rows_each, 0
    )
    entries = pl.pallas_call(
        functools.partial(relay_kernel, rows_each),
        out_shape=jax.ShapeDtypeStruct((size, 2 * rows_each, PAIR), F32),
        compiler_params=params,
        name="relay",
    )(arrived, pull, start)
    entries = lax.all_to_all(entries, "tm", split_axis=0, concat_axis=0, tiled=True)
    state = entries[:, :rows_each].reshape(PAIRS, HEAD_SIZE, PAIR)
    grad = entries[:, rows_each:].reshape(PAIRS, HEAD_SIZE, PAIR)
    small = pl.BlockSpec((group, HEAD_SIZE, PAIR), lambda i: (i, 0, 0))
    y_low = pl.pallas_call(
        output_kernel,
        grid=steps,
        in_specs=[small, block, block],
        out_specs=pl.BlockSpec((group * PAIR, frames), lambda i: (i, 0)),
        out_shape=jax.ShapeDtypeStruct((width, frames), BF16),
        compiler_params=params,
        cost_estimate=cost(1 << 28, 2 << 20),
        name="output",
    )(state, y0, yr)
    y_low = y_low.reshape(size, width // size, frames)
    y_mine = lax.all_to_all(y_low, "tm", split_axis=0, concat_axis=0, tiled=True)
    grad_r, grad_k, grad_v = pl.pallas_call(
        last_kernel,
        grid=steps,
        in_specs=[small, small] + [block] * 14,
        out_specs=[block] * 3,
        out_shape=[low] * 3,
        compiler_params=params,
        cost_estimate=cost(8 << 30, 8 << 20),
        name="last",
    )(state, grad, grad_y, values, u0, x0, p0, tb, gv, gvk, gra, gka, total, b, a, scale)
    loss_scale = 1.0 / math.sqrt(frames * size)
    y_mine = y_mine.swapaxes(0, 1).reshape(width // size, size * frames)
    grad_weight = (
        lax.dot_general(y_mine, everything, (((1,), (1,)), ((), ())), preferred_element_type=F32)
        * loss_scale
    )
    return grad_r, grad_k, grad_v, grad_weight


def solution(mesh):
    rows = P(("groups", "tm"), None)
    return jax.shard_map(
        local,
        mesh=mesh,
        in_specs=(rows,) * 6 + (P("groups", None, None), P(), P("tm", "groups")),
        out_specs=(rows,) * 4,
        check_vma=False,
    )
```

```python
import functools
import math

import jax
import jax.numpy as jnp
from jax import lax
from jax.experimental import pallas as pl
from jax.experimental.pallas import tpu as pltpu
from jax.sharding import PartitionSpec as P

HEAD_COUNT = 16
HEAD_SIZE = 64
PAIR = 2 * HEAD_SIZE
PAIRS = HEAD_COUNT // 2
F32 = jnp.float32
BF16 = jnp.bfloat16

NN = (((1,), (0,)), ((), ()))
NT = (((1,), (1,)), ((), ()))
TN = (((0,), (0,)), ((), ()))


def split(x):
    high = x.astype(BF16)
    return high, (x - high.astype(F32)).astype(BF16)


def dot1(a, b, dims):
    return lax.dot_general(a, b, dims, preferred_element_type=F32)


def dot3(a, b, dims):
    a = (a,) if not isinstance(a, tuple) and a.dtype == BF16 else a if isinstance(a, tuple) else split(a)
    b = (b,) if not isinstance(b, tuple) and b.dtype == BF16 else b if isinstance(b, tuple) else split(b)
    out = dot1(a[0], b[0], dims)
    if len(b) > 1:
        out = out + dot1(a[0], b[1], dims)
    if len(a) > 1:
        out = out + dot1(a[1], b[0], dims)
    return out


def iota(shape, dim):
    return lax.broadcasted_iota(jnp.int32, shape, dim)


def both(f, lane_low):
    return jnp.where(lane_low, f(0), f(1))


def pack(full, lane_low):
    return jnp.where(lane_low, full[:HEAD_SIZE], full[HEAD_SIZE:])


def unpack(packed, diagonal):
    return jnp.where(diagonal, jnp.concatenate([packed, packed], 0), 0.0)


def inverses(lower, row, col):
    size = row.shape[0]
    eye = jnp.where(row == col, 1.0, 0.0).astype(F32)
    step = 1
    out = None
    while step < size:
        inside = (row // (2 * step) == col // (2 * step)) & (row // step != col // step)
        off = [jnp.where(inside, m, 0.0) for m in lower]
        if out is None:
            out = [eye - m for m in off]
        else:
            halves = [split(t) for t in out]
            mid = [dot3(m, t, NN) for m, t in zip(off, halves)]
            out = [t - dot3(h, m, NN) for t, h, m in zip(out, halves, mid)]
        step *= 2
    return out


GROUP = 2


def one_less_exp(x):
    series = jnp.full_like(x, 1.0 / math.factorial(10))
    for n in range(9, 0, -1):
        series = series * x + 1.0 / math.factorial(n)
    return jnp.where(x > -0.5, -x * series, 1.0 - jnp.exp(x))


def row_scales(total):
    frames = total.shape[0]
    return total[frames // 2 - 1 : frames // 2], total[frames - 1 : frames]


def forward_kernel(rows_each, rec_ref, key_ref, val_ref, log_ref, kap_ref, rem_ref, pay_ref,
                   u_ref, x_ref, y_ref, yr_ref, tot_ref, ks_ref, a_ref, b_ref, k_ref,
                   t_ref, ak_ref, rb_ref, rk_ref):
    frames = rec_ref.shape[0]
    row, col = iota((frames, frames), 0), iota((frames, frames), 1)
    lane_low = iota((frames, PAIR), 1) < HEAD_SIZE
    low2 = jnp.concatenate([lane_low, lane_low], 1)
    pack_low = iota((HEAD_SIZE, PAIR), 1) < HEAD_SIZE
    prow, pcol = iota((PAIR, PAIR), 0), iota((PAIR, PAIR), 1)
    ones = jnp.where((prow // HEAD_SIZE) == (pcol // HEAD_SIZE), 1.0, 0.0).astype(BF16)
    tri = jnp.where(row >= col, 1.0, 0.0).astype(BF16)
    own2 = [jnp.concatenate([m, m], 0) for m in (lane_low, jnp.logical_not(lane_low))]
    strict, lax_tri = row > col, row >= col
    zero = jnp.zeros((), BF16)
    count = rec_ref.shape[1] // PAIR

    m_ab = []
    for pair in range(count):
        at = pl.ds(pair * PAIR, PAIR)
        log_low = log_ref[:, at]
        log_part = log_low.astype(F32)
        total = dot1(tri, log_low, NN)
        middle, last = row_scales(total)
        key_scale = jnp.sqrt(one_less_exp(log_part))
        raw = kap_ref[:, at].astype(F32)
        norm = dot3(raw * raw, ones, NN)
        a = raw / jnp.sqrt(norm + 1e-06)
        e_neg = jnp.exp(middle - total)
        a_mid = a * jnp.exp(total - log_part - middle)
        b_mid = rem_ref[:, at].astype(F32) * a * e_neg
        k_mid = key_ref[:, at].astype(F32) * key_scale * e_neg
        r_mid = rec_ref[:, at].astype(F32) * jnp.exp(total - middle)
        for ref, value in zip((tot_ref, ks_ref, a_ref, b_ref, k_ref), (total, key_scale, a_mid, b_mid, k_mid)):
            ref[:, at] = value
        upper = split(jnp.concatenate([a_mid, r_mid], 0))
        rights = split(jnp.concatenate([b_mid, k_mid], 0))
        for h, m in enumerate(own2):
            gram = dot3(upper, tuple(jnp.where(m, x, zero) for x in rights), NT)
            head = pl.ds((pair * 2 + h) * frames, frames)
            m_ab.append(jnp.where(strict, gram[:frames, :frames], 0.0))
            ak_ref[:, head] = jnp.where(strict, gram[:frames, frames:], 0.0)
            rb_ref[:, head] = jnp.where(lax_tri, gram[frames:, :frames], 0.0)
            rk_ref[:, head] = jnp.where(lax_tri, gram[frames:, frames:], 0.0)
    inverted = inverses(m_ab, row, col)

    for pair in range(count):
        at = pl.ds(pair * PAIR, PAIR)
        heads = [pl.ds((pair * 2 + h) * frames, frames) for h in range(2)]
        v = val_ref[:, at]
        total = tot_ref[:, at]
        middle, last = row_scales(total)
        a_abs = a_ref[:, at] * jnp.exp(middle)
        r_abs = rec_ref[:, at].astype(F32) * jnp.exp(total)
        scale = jnp.exp(last - middle)
        for h in range(2):
            t_ref[:, heads[h]] = inverted[pair * 2 + h]
        t_inv = [split(inverted[pair * 2 + h]) for h in range(2)]
        on_v = [dot3(jnp.concatenate([ak_ref[:, h], rk_ref[:, h]], 0), v, NN) for h in heads]
        on_v = jnp.where(own2[0], on_v[0], on_v[1])
        given = split(jnp.concatenate([on_v[:frames], a_abs], 1))
        inner = both(lambda h: dot3(t_inv[h], given, NN), low2)
        u_ref[:, at], x_ref[:, at] = inner[:, :PAIR], inner[:, PAIR:]
        inner = split(inner)
        minus = both(lambda h: dot3(rb_ref[:, heads[h]], inner, NN), low2)
        y_ref[:, at] = on_v[frames:] - minus[:, :PAIR]
        yr_ref[:, at] = r_abs - minus[:, PAIR:]
        ended = dot3(inner, b_ref[:, at] * scale, TN)
        through = pack(jnp.where(prow == pcol, jnp.exp(last), 0.0) - ended[PAIR:], pack_low)
        offset = pack(dot3(v, k_ref[:, at] * scale, TN) - ended[:PAIR], pack_low)
        for part in range(HEAD_SIZE // rows_each):
            to = pair * (HEAD_SIZE // rows_each) + part
            pay_ref[to, :HEAD_SIZE] = through
            pay_ref[to, HEAD_SIZE:] = offset[part * rows_each : (part + 1) * rows_each]


def backward_kernel(rows_each, rec_ref, val_ref, gy_ref, tot_ref, ks_ref, a_ref, b_ref, k_ref,
                    t_ref, ak_ref, rb_ref, rk_ref,
                    pay_ref, p_ref, tb_ref, gv_ref, gvk_ref, gra_ref, gka_ref):
    frames = rec_ref.shape[0]
    row, col = iota((frames, frames), 0), iota((frames, frames), 1)
    lane_low = iota((frames, PAIR), 1) < HEAD_SIZE
    own = [lane_low, jnp.logical_not(lane_low)]
    low2 = jnp.concatenate([lane_low, lane_low], 1)
    pack_low = iota((HEAD_SIZE, PAIR), 1) < HEAD_SIZE
    zero = jnp.zeros((), BF16)
    for pair in range(rec_ref.shape[1] // PAIR):
        at = pl.ds(pair * PAIR, PAIR)
        heads = [pl.ds((pair * 2 + h) * frames, frames) for h in range(2)]
        total = tot_ref[:, at]
        middle, last = row_scales(total)
        scale = jnp.exp(last - middle)
        v, q = val_ref[:, at], split(gy_ref[:, at])
        e_pos, e_neg = jnp.exp(total - middle), jnp.exp(middle - total)
        r = rec_ref[:, at].astype(F32)
        m_rb, m_rk, m_ak, t_inv = (
            [split(ref[:, h]) for h in heads] for ref in (rb_ref, rk_ref, ak_ref, t_ref)
        )
        back = both(lambda h: dot3(m_rb[h], q, TN), lane_low)
        given = split(jnp.concatenate([back, b_ref[:, at] * scale], 1))
        pulled = both(lambda h: dot3(t_inv[h], given, TN), low2)
        p0 = pulled[:, :PAIR]
        p_ref[:, at], tb_ref[:, at] = p0, pulled[:, PAIR:]
        pulled = split(pulled)
        minus = both(lambda h: dot3(m_ak[h], pulled, TN), low2)
        gv_ref[:, at] = both(lambda h: dot3(m_rk[h], q, TN), lane_low) - minus[:, :PAIR]
        gvk_ref[:, at] = k_ref[:, at] * scale - minus[:, PAIR:]
        v_own = [jnp.where(m, v, zero) for m in own]
        q_own = [tuple(jnp.where(m, x, zero) for x in q) for m in own]
        k_mid, r_mid = split(k_ref[:, at]), split(r * e_pos)
        gra_ref[:, at] = e_pos * both(
            lambda h: dot3(jnp.where(row >= col, dot3(q, v_own[h], NT), 0.0), k_mid, NN), lane_low
        )
        gka_ref[:, at] = ks_ref[:, at] * e_neg * both(
            lambda h: dot3(jnp.where(row <= col, dot3(v, q_own[h], NT), 0.0), r_mid, NN), lane_low
        )
        pull = dot3(q, r * jnp.exp(total), TN) - dot3(p0, a_ref[:, at] * jnp.exp(middle), TN)
        pull = pack(pull, pack_low)
        for part in range(HEAD_SIZE // rows_each):
            to = pair * (HEAD_SIZE // rows_each) + part
            pay_ref[to] = pull[part * rows_each : (part + 1) * rows_each]


def relay_kernel(rows_each, count, pay_ref, pull_ref, start_ref, state_out, grad_out,
                 held, local_sem, send_sem, recv_sem):
    me = lax.axis_index("tm")
    diagonal = (iota((PAIR, PAIR), 0) // HEAD_SIZE) == (iota((PAIR, PAIR), 1) // HEAD_SIZE)
    outs = (state_out, grad_out)
    barrier = pltpu.get_barrier_semaphore()

    def greet(i, carried):
        @pl.when(i != me)
        def _():
            pl.semaphore_signal(
                barrier, inc=1, device_id={"tm": i}, device_id_type=pl.DeviceIdType.MESH
            )

        return carried

    lax.fori_loop(0, count, greet, 0)
    pl.semaphore_wait(barrier, count - 1)

    def rows(i):
        return pl.ds(pl.multiple_of(i * rows_each, rows_each), rows_each)

    def remote(way, i, origin):
        return pltpu.make_async_remote_copy(
            src_ref=held.at[way, i],
            dst_ref=outs[way].at[rows(origin)],
            send_sem=send_sem.at[way, i],
            recv_sem=recv_sem.at[way, origin],
            device_id={"tm": i},
            device_id_type=pl.DeviceIdType.MESH,
        )

    def own(way):
        return pltpu.make_async_copy(held.at[way, me], outs[way].at[rows(me)], local_sem.at[way])

    def send(way, i):
        @pl.when(i != me)
        def _():
            remote(way, i, me).start()

        @pl.when(i == me)
        def _():
            own(way).start()

    def lap(i, carried):
        state, grad = carried
        j = count - 1 - i
        held[0, i] = state
        held[1, j] = grad
        state = pay_ref[i, HEAD_SIZE:] + dot3(state, unpack(pay_ref[i, :HEAD_SIZE], diagonal), NN)
        grad = pull_ref[j] + dot3(grad, unpack(pay_ref[j, :HEAD_SIZE], diagonal), NT)
        send(0, i)
        send(1, j)
        return state, grad

    lax.fori_loop(0, count, lap, (start_ref[...], jnp.zeros((rows_each, PAIR), F32)))

    def finish(i, carried):
        @pl.when(i != me)
        def _():
            for way in range(2):
                remote(way, i, me).wait_send()
                remote(way, i, i).wait_recv()

        return carried

    lax.fori_loop(0, count, finish, 0)
    own(0).wait()
    own(1).wait()


def output_kernel(state_ref, y_ref, yr_ref, ylow_ref):
    diagonal = (iota((PAIR, PAIR), 0) // HEAD_SIZE) == (iota((PAIR, PAIR), 1) // HEAD_SIZE)
    for pair in range(y_ref.shape[1] // PAIR):
        at = pl.ds(pair * PAIR, PAIR)
        state = unpack(state_ref[pair], diagonal)
        y = y_ref[:, at] + dot3(yr_ref[:, at], state, NT)
        ylow_ref[pl.ds(pair * PAIR, PAIR), :] = y.T.astype(BF16)


def last_kernel(state_ref, grad_ref, gy_ref, val_ref, u_ref, x_ref, p_ref, tb_ref,
                gv_ref, gvk_ref, gra_ref, gka_ref, tot_ref, b_ref, a_ref, ks_ref,
                gr_out, gk_out, gv_out):
    frames = gy_ref.shape[0]
    row, col = iota((frames, frames), 0), iota((frames, frames), 1)
    lane_low = iota((frames, PAIR), 1) < HEAD_SIZE
    own = [lane_low, jnp.logical_not(lane_low)]
    diagonal = (iota((PAIR, PAIR), 0) // HEAD_SIZE) == (iota((PAIR, PAIR), 1) // HEAD_SIZE)
    zero = jnp.zeros((), BF16)
    for pair in range(gy_ref.shape[1] // PAIR):
        at = pl.ds(pair * PAIR, PAIR)
        state = split(unpack(state_ref[pair], diagonal))
        grad = split(unpack(grad_ref[pair], diagonal))
        q, v = split(gy_ref[:, at]), val_ref[:, at]
        u = split(u_ref[:, at] + dot3(x_ref[:, at], state, NT))
        behind = dot3(jnp.concatenate([tb_ref[:, at], gvk_ref[:, at]], 0), grad, NT)
        p = split(p_ref[:, at] + behind[:frames])
        gv_out[:, at] = (gv_ref[:, at] + behind[frames:]).astype(BF16)
        b_mid, a_mid = split(b_ref[:, at]), split(a_ref[:, at])
        total = tot_ref[:, at]
        middle, last = total[frames // 2 - 1 : frames // 2], total[frames - 1 : frames]

        def removed(h):
            gram = dot3(q, tuple(jnp.where(own[h], x, zero) for x in u), NT)
            return dot3(jnp.where(row >= col, gram, 0.0), b_mid, NN)

        def removed_back(h):
            gram = dot3(v, tuple(jnp.where(own[h], x, zero) for x in p), NT)
            return dot3(jnp.where(row < col, gram, 0.0), a_mid, NN)

        gr = jnp.exp(total) * dot3(q, state, NN) + gra_ref[:, at]
        gr = gr - jnp.exp(total - middle) * both(removed, lane_low)
        gr_out[:, at] = gr.astype(BF16)
        gk = jnp.exp(last - total) * dot3(v, grad, NN) - jnp.exp(middle - total) * both(
            removed_back, lane_low
        )
        gk_out[:, at] = (gk * ks_ref[:, at] + gka_ref[:, at]).astype(BF16)


def cost(flops, moved):
    return pl.CostEstimate(flops=flops, bytes_accessed=moved, transcendentals=0)


def local(receptance, key_input, values, log_decay, kappa_raw, removal, initial_state, out_weight, grad_output):
    size = lax.axis_size("tm")
    frames, width = receptance.shape
    rows_each = PAIRS * HEAD_SIZE // size
    everything = lax.all_gather(grad_output, "tm", axis=0, tiled=True)
    gathered = lax.all_to_all(grad_output, "tm", split_axis=1, concat_axis=0, tiled=True)
    group = GROUP
    block = pl.BlockSpec((frames, group * PAIR), lambda i: (0, i))
    square = pl.BlockSpec((frames, group * 2 * frames), lambda i: (0, i))
    per_step = group * size // PAIRS
    flat = jax.ShapeDtypeStruct((frames, width), F32)
    matrix = jax.ShapeDtypeStruct((frames, HEAD_COUNT * frames), F32)
    low = jax.ShapeDtypeStruct((frames, width), BF16)
    params = pltpu.CompilerParams(vmem_limit_bytes=60 << 20)
    steps = (PAIRS // group,)

    def sent(rows):
        return (
            pl.BlockSpec((per_step, rows, PAIR), lambda i: (i, 0, 0)),
            jax.ShapeDtypeStruct((size, rows, PAIR), F32),
        )

    spec, shape = sent(HEAD_SIZE + rows_each)
    payload, u0, x0, y0, yr, total, scale, a, b, k, t, ak, rb, rk = pl.pallas_call(
        functools.partial(forward_kernel, rows_each),
        grid=steps,
        in_specs=[block] * 6,
        out_specs=[spec] + [block] * 9 + [square] * 4,
        out_shape=[shape] + [flat] * 9 + [matrix] * 4,
        compiler_params=params,
        cost_estimate=cost(20 << 30, 10 << 20),
        name="forward",
    )(receptance, key_input, values, log_decay, kappa_raw, removal)
    arrived = lax.all_to_all(payload, "tm", split_axis=0, concat_axis=0, tiled=True)
    grad_y = lax.dot_general(
        gathered, out_weight, (((0,), (1,)), ((), ())), preferred_element_type=F32
    )
    spec, shape = sent(rows_each)
    pull, p0, tb, gv, gvk, gra, gka = pl.pallas_call(
        functools.partial(backward_kernel, rows_each),
        grid=steps,
        in_specs=[block] * 8 + [square] * 4,
        out_specs=[spec] + [block] * 6,
        out_shape=[shape] + [flat] * 6,
        compiler_params=params,
        cost_estimate=cost(12 << 30, 10 << 20),
        name="backward",
    )(receptance, values, grad_y, total, scale, a, b, k, t, ak, rb, rk)
    arrived, pull = lax.optimization_barrier((arrived, pull))
    pull = lax.all_to_all(pull, "tm", split_axis=0, concat_axis=0, tiled=True)
    start = initial_state.reshape(PAIRS, 2, HEAD_SIZE, HEAD_SIZE).swapaxes(1, 2)
    start = lax.dynamic_slice_in_dim(
        start.reshape(PAIRS * HEAD_SIZE, PAIR), lax.axis_index("tm") * rows_each, rows_each, 0
    )
    whole = pl.BlockSpec(memory_space=pltpu.VMEM)
    anywhere = pl.BlockSpec(memory_space=pl.ANY)
    landed = jax.ShapeDtypeStruct((PAIRS * HEAD_SIZE, PAIR), F32)
    state, grad = pl.pallas_call(
        functools.partial(relay_kernel, rows_each, size),
        in_specs=[whole] * 3,
        out_specs=[anywhere] * 2,
        out_shape=[landed] * 2,
        scratch_shapes=[
            pltpu.VMEM((2, size, rows_each, PAIR), F32),
            pltpu.SemaphoreType.DMA((2,)),
            pltpu.SemaphoreType.DMA((2, size)),
            pltpu.SemaphoreType.DMA((2, size)),
        ],
        compiler_params=pltpu.CompilerParams(
            collective_id=0, has_side_effects=True, vmem_limit_bytes=32 << 20
        ),
        name="relay",
    )(arrived, pull, start)
    state = state.reshape(PAIRS, HEAD_SIZE, PAIR)
    grad = grad.reshape(PAIRS, HEAD_SIZE, PAIR)
    small = pl.BlockSpec((group, HEAD_SIZE, PAIR), lambda i: (i, 0, 0))
    y_low = pl.pallas_call(
        output_kernel,
        grid=steps,
        in_specs=[small, block, block],
        out_specs=pl.BlockSpec((group * PAIR, frames), lambda i: (i, 0)),
        out_shape=jax.ShapeDtypeStruct((width, frames), BF16),
        compiler_params=params,
        cost_estimate=cost(1 << 28, 2 << 20),
        name="output",
    )(state, y0, yr)
    y_low = y_low.reshape(size, width // size, frames)
    y_mine = lax.all_to_all(y_low, "tm", split_axis=0, concat_axis=0, tiled=True)
    grad_r, grad_k, grad_v = pl.pallas_call(
        last_kernel,
        grid=steps,
        in_specs=[small, small] + [block] * 14,
        out_specs=[block] * 3,
        out_shape=[low] * 3,
        compiler_params=params,
        cost_estimate=cost(8 << 30, 8 << 20),
        name="last",
    )(state, grad, grad_y, values, u0, x0, p0, tb, gv, gvk, gra, gka, total, b, a, scale)
    loss_scale = 1.0 / math.sqrt(frames * size)
    y_mine = y_mine.swapaxes(0, 1).reshape(width // size, size * frames)
    grad_weight = (
        lax.dot_general(y_mine, everything, (((1,), (1,)), ((), ())), preferred_element_type=F32)
        * loss_scale
    )
    return grad_r, grad_k, grad_v, grad_weight


def solution(mesh):
    rows = P(("groups", "tm"), None)
    return jax.shard_map(
        local,
        mesh=mesh,
        in_specs=(rows,) * 6 + (P("groups", None, None), P(), P("tm", "groups")),
        out_specs=(rows,) * 4,
        check_vma=False,
    )
```
